32 devices in a mesh: fsdp: 8 (over z, x), rep: 2 (over y), ctx: 2 (over core).
Axes of the slice: x: 2, y: 2, z: 4, core: 2. Of those that a mesh axis runs over, the one named last changes fastest.
Arguments:
- tokens: bfloat16 [16, 2048, 768], P(('fsdp', 'rep'), 'ctx'), may hold values from -10 to 10
- cotangent: bfloat16 [16, 2048, 768], P(('fsdp', 'rep'), 'ctx'), may hold values from -6 to 6
- doc_lengths: int32 [16, 4], P(('fsdp', 'rep')), may hold values from 1 to 1024, 2048 in all within a row
- attn_gain: bfloat16 [768], replicated, may hold values from 0.5 to 1.5
- qkv_weight: bfloat16 [768, 2304], P('fsdp'), may hold values from -1 to 1
- out_weight: bfloat16 [768, 768], P('fsdp'), may hold values from -1.75 to 1.75
- mlp_gain: bfloat16 [768], replicated, may hold values from 0.5 to 1.5
- in_weight: bfloat16 [768, 2304], P('fsdp'), may hold values from -0.21875 to 0.21875
- down_weight: bfloat16 [1152, 768], P('fsdp'), may hold values from -0.1875 to 0.1875
Outputs:
- output: bfloat16 [16, 2048, 768], P(('fsdp', 'rep'), 'ctx')
- input_grad: float32 [16, 2048, 768], P(('fsdp', 'rep'), 'ctx')
- grad_attn_gain: float32 [768], replicated
- grad_qkv: float32 [768, 2304], P('fsdp')
- grad_out: float32 [768, 768], P('fsdp')
- grad_mlp_gain: float32 [768], replicated
- grad_in: float32 [768, 2304], P('fsdp')
- grad_down: float32 [1152, 768], P('fsdp')
The draws below stay inside these ranges and needn't reach their ends.
Inputs may be any that keep to these rules, and one draw needn't show every extreme that they name: `doc_lengths`: the 4 lengths of a row sum to 2048; in every row the longest is exactly 1024.
All inputs are finite; a program needn't handle non-finite values.
Results may differ from the reference program's by a relative error of at most 0.038.
Values may be sent and summed in bfloat16 or wider, within the bound.
A program may use at most 256 MiB of HBM per device.

```python
import math
import jax
import jax.numpy as jnp
import numpy as np
from jax import lax

D = 768
FF = 1152
HEADS = 12
HD = 64
LEN = 2048
NDOC = 4
ROWS = 16


def draw_tokens(key, part):
    values = jax.random.truncated_normal(jax.random.fold_in(key, 11), -6.0, 6.0, (ROWS, LEN, D), jnp.float32)
    return values.astype(jnp.bfloat16)


def draw_qkv_weight(key, part):
    values = jax.random.truncated_normal(jax.random.fold_in(key, 21), -6.0, 6.0, (D, 3 * D), jnp.float32) * D ** (-0.5)
    return values.astype(jnp.bfloat16)


def shard_levels(rng, shape, cuts, least, high):
    factor_of, own = 1.0, jax.random.fold_in(rng, 6)
    for dim, shards_of in cuts:
        draws = jnp.exp(jax.random.uniform(jax.random.fold_in(own, dim), (shards_of,), jnp.float32, least / len(cuts), high / len(cuts)))
        factor_of = factor_of * jnp.repeat(draws, shape[dim] // shards_of).reshape([-1 if axis == dim else 1 for axis in range(len(shape))])
    return factor_of


def split_up(count, total, limit, lean):
    loads = [(1 << 20) // math.isqrt(rank ** lean) + 1 for rank in range(2, count + 1)]
    rest, given = total - limit - (count - 1), [1] * (count - 1)
    while rest > 0:
        free = [i for i in range(count - 1) if given[i] < limit]
        pool, left = sum([loads[i] for i in free]), rest
        for i in free:
            more = min(limit - given[i], max(1, left * loads[i] // pool), rest)
            given[i] = given[i] + more
            rest = rest - more
    return np.array([limit] + given)


def ragged(rng, number_of, total, limit, slope):
    if number_of == 2:
        one = jax.random.randint(rng, (), max(1, total - limit), min(limit, total - 1) + 1)
        return jnp.stack([one, total - one])
    tallies = jnp.asarray(split_up(number_of, total, limit, slope), jnp.int32)
    couples = (number_of - 1) // 2
    giver, sink = tallies[1:1 + 2 * couples:2], tallies[2:2 + 2 * couples:2]
    room = jnp.minimum(giver - 1, limit - sink)
    passed = jax.random.randint(jax.random.fold_in(rng, 1), (couples,), 0, 1 << 20) % (room + 1)
    tallies = tallies.at[1:1 + 2 * couples:2].set(giver - passed).at[2:2 + 2 * couples:2].set(sink + passed)
    return tallies[jax.random.permutation(jax.random.fold_in(rng, 2), number_of)]


def centred(stream_key, shape, scale, most, pieces=(), held_as=jnp.bfloat16):
    drawn = scale * jax.random.normal(stream_key, shape, jnp.float32)
    if pieces:
        drawn = drawn * shard_levels(stream_key, shape, pieces, -0.22, 0.18)
    return jnp.clip(drawn, -most, most).astype(held_as)


def setup_inputs(seed: int = 0) -> dict:
    seeds = jax.random.split(jax.random.key(seed), 10)
    return {
        "tokens": draw_tokens(jax.random.fold_in(seeds[9], 71), 0),
        "cotangent": centred(seeds[1], (ROWS, LEN, D), 1.0, 6.0, ((0, 16), (1, 2))),
        "doc_lengths": jax.vmap(lambda own: ragged(own, NDOC, LEN, LEN // 2, 1))(jax.random.split(seeds[2], ROWS)).reshape((ROWS, NDOC)).astype(jnp.int32),
        "attn_gain": jnp.clip(1.0 + 0.1 * jax.random.normal(seeds[3], (D,), jnp.float32), 0.5, 1.5).astype(jnp.bfloat16),
        "qkv_weight": draw_qkv_weight(jax.random.fold_in(seeds[9], 71), 0),
        "out_weight": centred(seeds[5], (D, D), (D // 64) ** -0.5, 1.75, ((0, 8),)),
        "mlp_gain": jnp.clip(1.0 + 0.1 * jax.random.normal(seeds[6], (D,), jnp.float32), 0.5, 1.5).astype(jnp.bfloat16),
        "in_weight": centred(seeds[7], (D, 2 * FF), D ** -0.5, 0.21875, ((0, 8),)),
        "down_weight": centred(seeds[8], (FF, D), FF ** -0.5, 0.1875, ((0, 8),)),
    }


norm_eps = 1e-05
rope_base = 160000.0
masked_score = -1e+30

def to_half(values):
    return lax.optimization_barrier(values.astype(jnp.bfloat16))

def layer_norm(values):
    center = values - lax.optimization_barrier(jnp.mean(values, axis=-1, keepdims=True))
    inverse = lax.rsqrt(lax.optimization_barrier(jnp.mean(center * center, axis=-1, keepdims=True)) + norm_eps)
    return (center * inverse, inverse)

def norm_back(grad_normed, normed, inverse):
    mean_grad = lax.optimization_barrier(jnp.mean(grad_normed, axis=-1, keepdims=True))
    mean_cross = lax.optimization_barrier(jnp.mean(grad_normed * normed, axis=-1, keepdims=True))
    return (grad_normed - mean_grad - normed * mean_cross) * inverse

def gelu_pair(values):
    cumulative = 0.5 * (1.0 + lax.erf(values * 0.7071067811865476))
    density = jnp.exp(-0.5 * values * values) * 0.3989422804014327
    return (values * cumulative, cumulative + values * density)

def doc_tables(lengths, positions):
    doc_ends = jnp.cumsum(lengths).astype(jnp.int32)
    before = (doc_ends[None, :] <= positions[:, None]).astype(jnp.int32)
    segment = lax.optimization_barrier(jnp.sum(before, axis=1)).astype(jnp.int32)
    begins = lax.optimization_barrier(jnp.sum(before * lengths[None, :], axis=1)).astype(jnp.int32)
    return (segment, positions - begins)

def rope_tables(offsets, head_size):
    half_size = head_size // 2
    frequency = rope_base ** (-(jnp.arange(half_size, dtype=jnp.float32) * (2.0 / head_size)))
    angles = offsets.astype(jnp.float32)[..., None] * frequency
    return (jnp.cos(angles), jnp.sin(angles))

def rotate(values, cosine, sine_part):
    half_size = values.shape[-1] // 2
    leading, trailing = (values[..., :half_size], values[..., half_size:])
    cos_head, sin_head = (cosine[..., None, :], sine_part[..., None, :])
    return jnp.concatenate([leading * cos_head - trailing * sin_head, trailing * cos_head + leading * sin_head], axis=-1)

def unrotate(gradient, cosine, sine_part):
    half_size = gradient.shape[-1] // 2
    leading, trailing = (gradient[..., :half_size], gradient[..., half_size:])
    cos_head, sin_head = (cosine[..., None, :], sine_part[..., None, :])
    return jnp.concatenate([leading * cos_head + trailing * sin_head, trailing * cos_head - leading * sin_head], axis=-1)

def attend_row(query, key_half, value_half, segment, score_scale, block_rows):
    key_wide = key_half.astype(jnp.float32)
    value_wide = value_half.astype(jnp.float32)

    def one_block(index):
        rows_query = lax.dynamic_slice_in_dim(query, index * block_rows, block_rows, 0).astype(jnp.float32)
        seg_query = lax.dynamic_slice_in_dim(segment, index * block_rows, block_rows, 0)
        scores = jnp.einsum('qhd,khd->hqk', rows_query, key_wide) * score_scale
        allowed = (seg_query[:, None] == segment[None, :])[None]
        scores = jnp.where(allowed, scores, masked_score)
        top_score = lax.optimization_barrier(jnp.max(scores, axis=-1, keepdims=True))
        weights = jnp.where(allowed, jnp.exp(scores - top_score), 0.0)
        running = lax.optimization_barrier(jnp.sum(weights, axis=-1))
        weights_half = to_half(weights).astype(jnp.float32)
        unscaled = jnp.einsum('hqk,khd->qhd', weights_half, value_wide)
        attended = unscaled / jnp.transpose(running)[:, :, None]
        return (attended, top_score[..., 0] + jnp.log(running))
    attended, log_total = lax.map(one_block, jnp.arange(LEN // block_rows, dtype=jnp.int32))
    return (attended.reshape(LEN, HEADS, HD), log_total)

def attend_back_row(query, key_half, value_half, attended, d_att, log_total, segment, score_scale, block_rows):
    key_wide = key_half.astype(jnp.float32)
    value_wide = value_half.astype(jnp.float32)

    def one_block(carry, index):
        key_grad, value_grad = carry
        first_row = index * block_rows
        rows_query = lax.dynamic_slice_in_dim(query, first_row, block_rows, 0).astype(jnp.float32)
        rows_out = lax.dynamic_slice_in_dim(attended, first_row, block_rows, 0).astype(jnp.float32)
        rows_grad = lax.dynamic_slice_in_dim(d_att, first_row, block_rows, 0).astype(jnp.float32)
        seg_query = lax.dynamic_slice_in_dim(segment, first_row, block_rows, 0)
        scores = jnp.einsum('qhd,khd->hqk', rows_query, key_wide) * score_scale
        allowed = (seg_query[:, None] == segment[None, :])[None]
        block_total = lax.dynamic_index_in_dim(log_total, index, 0, keepdims=False)
        probs = jnp.where(allowed, jnp.exp(scores - block_total[..., None]), 0.0)
        d_probs = jnp.einsum('qhd,khd->hqk', rows_grad, value_wide)
        delta = jnp.transpose(lax.optimization_barrier(jnp.sum(rows_grad * rows_out, axis=-1)))[:, :, None]
        d_scores = to_half(probs * (d_probs - delta)).astype(jnp.float32)
        probs_half = to_half(probs).astype(jnp.float32)
        query_grad = jnp.einsum('hqk,khd->qhd', d_scores, key_wide) * score_scale
        key_grad = key_grad + jnp.einsum('hqk,qhd->khd', d_scores, rows_query) * score_scale
        value_grad = value_grad + jnp.einsum('hqk,qhd->khd', probs_half, rows_grad)
        return ((key_grad, value_grad), query_grad)
    zero_grad = jnp.zeros((LEN, HEADS, HD), jnp.float32)
    (key_grad, value_grad), query_grad = lax.scan(one_block, (zero_grad, zero_grad), jnp.arange(LEN // block_rows, dtype=jnp.int32))
    return (query_grad.reshape(LEN, HEADS, HD), key_grad, value_grad)

def row_pass(x_row, cot_row, lengths, attn_gain, qkv_weight, out_weight, mlp_gain, in_weight, down_weight):
    score_scale = HD ** (-0.5)
    block_rows = min(512, LEN)
    positions = jnp.arange(LEN, dtype=jnp.int32)
    segment, offsets = doc_tables(lengths, positions)
    cosine, sine_part = rope_tables(offsets, HD)
    inputs = x_row.astype(jnp.float32)
    normed_attn, inverse_attn = layer_norm(inputs)
    act_attn = to_half(normed_attn * attn_gain.astype(jnp.float32))
    qkv_all = jnp.dot(act_attn, qkv_weight, preferred_element_type=jnp.float32)
    query = to_half(rotate(qkv_all[:, :D].reshape(LEN, HEADS, HD), cosine, sine_part))
    key_half = to_half(rotate(qkv_all[:, D:2 * D].reshape(LEN, HEADS, HD), cosine, sine_part))
    value_half = to_half(qkv_all[:, 2 * D:].reshape(LEN, HEADS, HD))
    attended, log_total = attend_row(query, key_half, value_half, segment, score_scale, block_rows)
    attended = to_half(attended)
    att_flat = attended.reshape(LEN, D)
    residual = inputs + jnp.dot(att_flat, out_weight, preferred_element_type=jnp.float32)
    normed_mlp, inverse_mlp = layer_norm(residual)
    act_mlp = to_half(normed_mlp * mlp_gain.astype(jnp.float32))
    up_all = jnp.dot(act_mlp, in_weight, preferred_element_type=jnp.float32)
    inner, gate = (up_all[:, :FF], up_all[:, FF:])
    gelu_value, gelu_slope = gelu_pair(inner)
    mixed = to_half(gelu_value * gate)
    output = (residual + jnp.dot(mixed, down_weight, preferred_element_type=jnp.float32)).astype(jnp.bfloat16)
    grad_down = jnp.dot(mixed.T, cot_row, preferred_element_type=jnp.float32)
    d_mixed = jnp.dot(cot_row, down_weight.T, preferred_element_type=jnp.float32)
    d_up = to_half(jnp.concatenate([d_mixed * gate * gelu_slope, d_mixed * gelu_value], axis=-1))
    grad_in = jnp.dot(act_mlp.T, d_up, preferred_element_type=jnp.float32)
    d_act_mlp = jnp.dot(d_up, in_weight.T, preferred_element_type=jnp.float32)
    grad_mlp_gain = lax.optimization_barrier(jnp.sum(d_act_mlp * normed_mlp, axis=0))
    d_residual = cot_row.astype(jnp.float32) + norm_back(d_act_mlp * mlp_gain.astype(jnp.float32), normed_mlp, inverse_mlp)
    d_res_half = to_half(d_residual)
    grad_out = jnp.dot(att_flat.T, d_res_half, preferred_element_type=jnp.float32)
    d_att = to_half(jnp.dot(d_res_half, out_weight.T, preferred_element_type=jnp.float32)).reshape(LEN, HEADS, HD)
    query_grad, key_grad, value_grad = attend_back_row(query, key_half, value_half, attended, d_att, log_total, segment, score_scale, block_rows)
    query_grad = unrotate(query_grad, cosine, sine_part).reshape(LEN, D)
    key_grad = unrotate(key_grad, cosine, sine_part).reshape(LEN, D)
    d_qkv = to_half(jnp.concatenate([query_grad, key_grad, value_grad.reshape(LEN, D)], axis=-1))
    grad_qkv = jnp.dot(act_attn.T, d_qkv, preferred_element_type=jnp.float32)
    d_act_attn = jnp.dot(d_qkv, qkv_weight.T, preferred_element_type=jnp.float32)
    grad_attn_gain = lax.optimization_barrier(jnp.sum(d_act_attn * normed_attn, axis=0))
    input_grad = d_residual + norm_back(d_act_attn * attn_gain.astype(jnp.float32), normed_attn, inverse_attn)
    return (output, input_grad, (grad_attn_gain, grad_qkv, grad_out, grad_mlp_gain, grad_in, grad_down))

def reference(tokens, cotangent, doc_lengths, attn_gain, qkv_weight, out_weight, mlp_gain, in_weight, down_weight):

    def row_step(carry, row_data):
        x_row, cot_row, lengths = row_data
        output, input_grad, grads = row_pass(x_row, cot_row, lengths, attn_gain, qkv_weight, out_weight, mlp_gain, in_weight, down_weight)
        summed = tuple((running + addend for running, addend in zip(carry, grads)))
        return (summed, (output, input_grad))
    initial = (jnp.zeros((D,), jnp.float32), jnp.zeros((D, 3 * D), jnp.float32), jnp.zeros((D, D), jnp.float32), jnp.zeros((D,), jnp.float32), jnp.zeros((D, 2 * FF), jnp.float32), jnp.zeros((FF, D), jnp.float32))
    grads, (output, input_grad) = lax.scan(row_step, initial, (tokens, cotangent, doc_lengths))
    return (output, input_grad, grads[0], grads[1], grads[2], grads[3], grads[4], grads[5])
```

```python
import functools

import jax
import jax.numpy as jnp
from jax import lax
from jax.experimental import pallas as pl
from jax.experimental.pallas import tpu as pltpu
from jax.sharding import PartitionSpec as P

HD = 64
PAIR = 2 * HD

norm_eps = 1e-05
rope_base = 160000.0
masked_score = -1e30
QB = 256
KB = 256
bf16 = jnp.bfloat16
f32 = jnp.float32
NT = (((1,), (1,)), ((), ()))


def params(count):
    return pltpu.CompilerParams(
        dimension_semantics=("arbitrary",) * count, vmem_limit_bytes=56 * 1024 * 1024
    )


def layer_norm(values):
    center = values - jnp.mean(values, axis=-1, keepdims=True)
    inverse = lax.rsqrt(jnp.mean(center * center, axis=-1, keepdims=True) + norm_eps)
    return (center * inverse, inverse)


def norm_back(grad_normed, normed, inverse):
    mean_grad = jnp.mean(grad_normed, axis=-1, keepdims=True)
    mean_cross = jnp.mean(grad_normed * normed, axis=-1, keepdims=True)
    return (grad_normed - mean_grad - normed * mean_cross) * inverse


def gelu_pair(values):
    cumulative = 0.5 * (1.0 + lax.erf(values * 0.7071067811865476))
    density = jnp.exp(-0.5 * values * values) * 0.3989422804014327
    return (values * cumulative, cumulative + values * density)


def doc_tables(lengths, positions):
    doc_ends = jnp.cumsum(lengths)
    before = (doc_ends[None, :] <= positions[:, None]).astype(jnp.int32)
    segment = jnp.sum(before, axis=1)
    begins = jnp.sum(before * lengths[None, :], axis=1)
    return (segment, positions - begins)


def rope_lanes(offsets):
    lane = jnp.arange(PAIR, dtype=jnp.int32) % HD
    frequency = rope_base ** (-((lane % (HD // 2)).astype(f32) * (2.0 / HD)))
    angles = offsets.astype(f32)[:, None] * frequency
    sign = jnp.where(lane < HD // 2, -1.0, 1.0).astype(f32)
    return (jnp.cos(angles), jnp.sin(angles) * sign)


def swap_halves(values):
    lane = lax.broadcasted_iota(jnp.int32, values.shape, 1)
    front = (lane % HD) < HD // 2
    return jnp.where(
        front,
        pltpu.roll(values, PAIR - HD // 2, 1),
        pltpu.roll(values, HD // 2, 1),
    )


def qkv_kernel(x_ref, gain_ref, cos_ref, sin_ref, w_ref, act_ref, q_ref, kv_ref):
    width = x_ref.shape[1]
    normed, _ = layer_norm(x_ref[...].astype(f32))
    act = (normed * gain_ref[...].astype(f32)).astype(bf16)
    act_ref[...] = act
    cosine, sine = cos_ref[...], sin_ref[...]
    for start in range(0, 3 * width, 2 * PAIR):
        part = jnp.dot(act, w_ref[:, start : start + 2 * PAIR], preferred_element_type=f32)
        for half in range(2):
            at = start + half * PAIR
            piece = part[:, half * PAIR : (half + 1) * PAIR]
            if at < 2 * width:
                piece = piece * cosine + swap_halves(piece) * sine
            if at < width:
                q_ref[:, at : at + PAIR] = piece.astype(bf16)
            else:
                kv_ref[:, at - width : at - width + PAIR] = piece.astype(bf16)


def qkv_call(inputs, gain, cosine, sine, weight):
    count, width = inputs.shape
    rows = min(256, count)
    row = lambda n: pl.BlockSpec((rows, n), lambda i: (i, 0))
    whole = lambda a: pl.BlockSpec(a.shape, lambda i: (0, 0))
    return pl.pallas_call(
        qkv_kernel,
        grid=(count // rows,),
        in_specs=[row(width), whole(gain), row(PAIR), row(PAIR), whole(weight)],
        out_specs=[row(width), row(width), row(2 * width)],
        out_shape=[
            jax.ShapeDtypeStruct((count, width), bf16),
            jax.ShapeDtypeStruct((count, width), bf16),
            jax.ShapeDtypeStruct((count, 2 * width), bf16),
        ],
        compiler_params=params(1),
        cost_estimate=pl.CostEstimate(
            flops=6 * count * width * width, bytes_accessed=12 * 1024 * 1024, transcendentals=0
        ),
    )(inputs, gain, cosine, sine, weight)


def split_heads(values, mark):
    lane = lax.broadcasted_iota(jnp.int32, values.shape, 1)
    zero = jnp.zeros_like(values)
    front, back = jnp.where(lane < HD, values, zero), jnp.where(lane < HD, zero, values)
    if mark is None:
        return front, back
    return jnp.concatenate([front, mark], axis=1), jnp.concatenate([back, mark], axis=1)


def fwd_kernel(step, lo_ref, hi_ref, q_ref, k_ref, v_ref, qm_ref, km_ref, o_ref, lse_ref, vt_ref):
    r, block = pl.program_id(0), pl.program_id(2)
    scale = HD ** (-0.5)

    @pl.when(block == 0)
    def _():
        for i in range(vt_ref.shape[0]):
            vt_ref[i] = v_ref[0, i * step : (i + 1) * step, :].T

    queries = split_heads((q_ref[0].astype(f32) * scale).astype(bf16), qm_ref[0])
    count = q_ref.shape[1]

    def body(index, carry):
        rows = pl.ds(pl.multiple_of(index * step, step), step)
        keys = jnp.concatenate([k_ref[0, rows, :], km_ref[0, rows, :]], axis=1)
        turned = vt_ref[index]
        result = []
        for h in range(2):
            run_max, run_sum, accum = carry[h]
            scores = lax.dot_general(keys, queries[h], NT, preferred_element_type=f32)
            new_max = jnp.maximum(run_max, jnp.max(scores, axis=0, keepdims=True))
            weights = jnp.exp(scores - new_max)
            factor = jnp.exp(run_max - new_max)
            new_sum = run_sum * factor + jnp.sum(weights, axis=0, keepdims=True)
            new_acc = accum * factor + jnp.dot(
                turned[h * HD : (h + 1) * HD], weights.astype(bf16), preferred_element_type=f32
            )
            result.append((new_max, new_sum, new_acc))
        return tuple(result)

    one = (
        jnp.full((1, count), masked_score, f32),
        jnp.zeros((1, count), f32),
        jnp.zeros((HD, count), f32),
    )
    state = lax.fori_loop(lo_ref[r, block], hi_ref[r, block], body, (one, one))
    outs = []
    for h in range(2):
        run_max, run_sum, accum = state[h]
        lse_ref[0, 0, h : h + 1, :] = run_max + jnp.log(run_sum)
        outs.append(accum / run_sum)
    o_ref[0] = jnp.concatenate(outs, axis=0).T.astype(bf16)


def fwd_call(lo, hi, query, kv, qmark, kmark, step):
    rows_here, count, width = query.shape
    length = kv.shape[1]
    pairs = width // PAIR
    qb = count // lo.shape[1]
    qspec = pl.BlockSpec((1, qb, PAIR), lambda r, h, i, *_: (r, i, h))
    return pl.pallas_call(
        functools.partial(fwd_kernel, step),
        grid_spec=pltpu.PrefetchScalarGridSpec(
            num_scalar_prefetch=2,
            grid=(rows_here, pairs, count // qb),
            in_specs=[
                qspec,
                pl.BlockSpec((1, length, PAIR), lambda r, h, i, *_: (r, 0, h)),
                pl.BlockSpec((1, length, PAIR), lambda r, h, i, *_: (r, 0, h + pairs)),
                pl.BlockSpec((1, qb, PAIR), lambda r, h, i, *_: (r, i, 0)),
                pl.BlockSpec((1, length, PAIR), lambda r, h, i, *_: (r, 0, 0)),
            ],
            out_specs=[
                qspec,
                pl.BlockSpec((1, 1, 2, qb), lambda r, h, i, *_: (r, h, 0, i)),
            ],
            scratch_shapes=[pltpu.VMEM((length // step, PAIR, step), bf16)],
        ),
        out_shape=[
            jax.ShapeDtypeStruct(query.shape, bf16),
            jax.ShapeDtypeStruct((rows_here, pairs, 2, count), f32),
        ],
        compiler_params=params(3),
        cost_estimate=pl.CostEstimate(
            flops=rows_here * 8 * count * length * width,
            bytes_accessed=16 * 1024 * 1024,
            transcendentals=0,
        ),
    )(lo, hi, query, kv, kv, qmark, kmark)


def bwd_kernel(
    step, lo_ref, hi_ref, q_ref, k_ref, v_ref, qm_ref, km_ref, do_ref, o_ref, lse_ref,
    cos_ref, sin_ref, dq_ref, dkv_ref, kt_ref, dk_acc, dv_acc,
):
    r, block = pl.program_id(0), pl.program_id(2)
    scale = HD ** (-0.5)

    @pl.when(block == 0)
    def _():
        for i in range(kt_ref.shape[0]):
            kt_ref[i] = k_ref[0, i * step : (i + 1) * step, :].T
        dk_acc[...] = jnp.zeros_like(dk_acc)
        dv_acc[...] = jnp.zeros_like(dv_acc)

    count = q_ref.shape[1]
    scaled = (q_ref[0].astype(f32) * scale).astype(bf16)
    queries = split_heads(scaled, qm_ref[0])
    query_rows = jnp.concatenate(split_heads(scaled, None), axis=0)
    grads = split_heads(do_ref[0], None)
    grad_rows = jnp.concatenate(grads, axis=0)
    products = (do_ref[0].astype(f32) * o_ref[0].astype(f32)).T
    deltas = [jnp.sum(products[h * HD : (h + 1) * HD], axis=0, keepdims=True) for h in range(2)]
    totals = [lse_ref[0, 0, h : h + 1, :] for h in range(2)]

    def body(index, carry):
        rows = pl.ds(pl.multiple_of(index * step, step), step)
        keys = jnp.concatenate([k_ref[0, rows, :], km_ref[0, rows, :]], axis=1)
        values = v_ref[0, rows, :]
        turned = kt_ref[index]
        result, probs_all, ds_all = [], [], []
        for h in range(2):
            scores = lax.dot_general(keys, queries[h], NT, preferred_element_type=f32)
            probs = jnp.exp(scores - totals[h])
            d_probs = lax.dot_general(values, grads[h], NT, preferred_element_type=f32)
            d_scores = (probs * (d_probs - deltas[h])).astype(bf16)
            result.append(
                carry[h]
                + jnp.dot(turned[h * HD : (h + 1) * HD], d_scores, preferred_element_type=f32)
            )
            probs_all.append(probs.astype(bf16))
            ds_all.append(d_scores)
        dv_acc[rows, :] += jnp.dot(
            jnp.concatenate(probs_all, axis=1), grad_rows, preferred_element_type=f32
        )
        dk_acc[rows, :] += jnp.dot(
            jnp.concatenate(ds_all, axis=1), query_rows, preferred_element_type=f32
        )
        return tuple(result)

    zero = jnp.zeros((HD, count), f32)
    state = lax.fori_loop(lo_ref[r, block], hi_ref[r, block], body, (zero, zero))
    d_query = jnp.concatenate(state, axis=0).T * scale
    d_query = d_query * cos_ref[0] - swap_halves(d_query) * sin_ref[0]
    dq_ref[0] = d_query.astype(bf16)

    @pl.when(block == pl.num_programs(2) - 1)
    def _():
        dkv_ref[0, 0] = dk_acc[...].astype(bf16)
        dkv_ref[1, 0] = dv_acc[...].astype(bf16)


def bwd_call(lo, hi, query, kv, qmark, kmark, d_att, att, lse, cosine, sine, step):
    rows_here, count, width = query.shape
    length = kv.shape[1]
    pairs = width // PAIR
    qb = count // lo.shape[1]
    qspec = pl.BlockSpec((1, qb, PAIR), lambda r, h, i, *_: (r, i, h))
    tspec = pl.BlockSpec((1, qb, PAIR), lambda r, h, i, *_: (r, i, 0))
    return pl.pallas_call(
        functools.partial(bwd_kernel, step),
        grid_spec=pltpu.PrefetchScalarGridSpec(
            num_scalar_prefetch=2,
            grid=(rows_here, pairs, count // qb),
            in_specs=[
                qspec,
                pl.BlockSpec((1, length, PAIR), lambda r, h, i, *_: (r, 0, h)),
                pl.BlockSpec((1, length, PAIR), lambda r, h, i, *_: (r, 0, h + pairs)),
                tspec,
                pl.BlockSpec((1, length, PAIR), lambda r, h, i, *_: (r, 0, 0)),
                qspec,
                qspec,
                pl.BlockSpec((1, 1, 2, qb), lambda r, h, i, *_: (r, h, 0, i)),
                tspec,
                tspec,
            ],
            out_specs=[
                qspec,
                pl.BlockSpec((2, 1, length, PAIR), lambda r, h, i, *_: (0, r, 0, h)),
            ],
            scratch_shapes=[
                pltpu.VMEM((length // step, PAIR, step), bf16),
                pltpu.VMEM((length, PAIR), f32),
                pltpu.VMEM((length, PAIR), f32),
            ],
        ),
        out_shape=[
            jax.ShapeDtypeStruct(query.shape, bf16),
            jax.ShapeDtypeStruct((2, rows_here, length, width), bf16),
        ],
        compiler_params=params(3),
        cost_estimate=pl.CostEstimate(
            flops=rows_here * 20 * count * length * width,
            bytes_accessed=24 * 1024 * 1024,
            transcendentals=0,
        ),
    )(lo, hi, query, kv, kv, qmark, kmark, d_att, att, lse, cosine, sine)


def join_kernel(parts, *refs):
    dq_ref, cos_ref, sin_ref = refs[:3]
    sides, out_ref = refs[3:-1], refs[-1]
    width = dq_ref.shape[1]
    out_ref[:, :width] = dq_ref[...]
    for at in range(0, width, PAIR):
        lanes = slice(at, at + PAIR)
        d_key = sum(s[0, :, lanes].astype(f32) for s in sides)
        d_key = d_key * cos_ref[...] - swap_halves(d_key) * sin_ref[...]
        out_ref[:, width + at : width + at + PAIR] = d_key.astype(bf16)
        d_value = sum(s[1, :, lanes].astype(f32) for s in sides)
        out_ref[:, 2 * width + at : 2 * width + at + PAIR] = d_value.astype(bf16)


def join_call(dq, cosine, sine, sides):
    count, width = dq.shape
    rows = min(256, count)
    row = lambda n: pl.BlockSpec((rows, n), lambda i: (i, 0))
    return pl.pallas_call(
        functools.partial(join_kernel, len(sides)),
        grid=(count // rows,),
        in_specs=[row(width), row(PAIR), row(PAIR)]
        + [pl.BlockSpec((2, rows, width), lambda i: (0, i, 0))] * len(sides),
        out_specs=row(3 * width),
        out_shape=jax.ShapeDtypeStruct((count, 3 * width), bf16),
        compiler_params=params(1),
        cost_estimate=pl.CostEstimate(
            flops=count * width * 10, bytes_accessed=12 * 1024 * 1024, transcendentals=0
        ),
    )(dq, cosine, sine, *sides)


def token_grad(activations, gradient):
    return lax.dot_general(
        activations, gradient, (((0,), (0,)), ((), ())), preferred_element_type=f32
    ).astype(bf16)


def matmul_back(gradient, weight):
    return lax.dot_general(gradient, weight, NT, preferred_element_type=f32)


def per_device(
    sizes,
    tokens,
    cotangent,
    doc_lengths,
    attn_gain,
    qkv_weight,
    out_weight,
    mlp_gain,
    in_weight,
    down_weight,
):
    rows_here, block_len, width = tokens.shape
    ctx_size = sizes["ctx"]
    length = block_len * ctx_size
    flat_count = rows_here * block_len
    hidden = down_weight.shape[0] * sizes["fsdp"]
    docs = doc_lengths.shape[1]

    def pair_sum(value, axis):
        if sizes[axis] == 2:
            other = lax.ppermute(value, axis, [(0, 1), (1, 0)])
            return value.astype(f32) + other.astype(f32)
        return lax.psum(value, axis).astype(f32)

    def gather(weight):
        return lax.all_gather(weight, "fsdp", axis=0, tiled=True)

    def scatter(grad):
        return lax.psum_scatter(grad, "fsdp", scatter_dimension=0, tiled=True)

    def replica_sum(shard):
        return pair_sum(pair_sum(shard, "ctx").astype(bf16), "rep")

    ctx_index = lax.axis_index("ctx")
    first_pos = ctx_index * block_len
    local_pos = first_pos + jnp.arange(block_len, dtype=jnp.int32)
    all_pos = jnp.arange(length, dtype=jnp.int32)
    seg_all, _ = jax.vmap(doc_tables, in_axes=(0, None))(doc_lengths, all_pos)
    seg_query, offsets = jax.vmap(doc_tables, in_axes=(0, None))(doc_lengths, local_pos)
    cosine, sine = rope_lanes(offsets.reshape(flat_count))
    lane = jnp.arange(PAIR, dtype=jnp.int32)
    qmark = (seg_query[:, :, None] == lane).astype(bf16)
    kmark = jnp.where(
        (seg_all[:, :, None] != lane) & (lane < docs), masked_score, 0.0
    ).astype(bf16)
    qb = min(QB, block_len)
    step = min(KB, length)
    ends = jnp.cumsum(doc_lengths, axis=1)
    low_pos = first_pos + jnp.arange(block_len // qb, dtype=jnp.int32) * qb
    high_pos = low_pos + qb - 1
    past = lambda pos: ends[:, None, :] <= pos[None, :, None]
    lo = jnp.max(jnp.where(past(low_pos), ends[:, None, :], 0), axis=-1) // step
    hi = jnp.min(jnp.where(past(high_pos), length, ends[:, None, :]), axis=-1)
    hi = (hi + step - 1) // step

    inputs_half = tokens.reshape(flat_count, width)
    full_qkv = gather(qkv_weight)
    act_attn, query, kv_local = qkv_call(
        inputs_half, attn_gain.reshape(1, width), cosine, sine, full_qkv
    )
    shaped = (rows_here, block_len, width)
    query = query.reshape(shaped)
    kv_local = kv_local.reshape(rows_here, block_len, 2 * width)
    if ctx_size == 2:
        kv_other = lax.ppermute(kv_local, "ctx", [(0, 1), (1, 0)])
        first = ctx_index == 0
        kv_all = jnp.concatenate(
            [jnp.where(first, kv_local, kv_other), jnp.where(first, kv_other, kv_local)], axis=1
        )
    else:
        kv_all = lax.all_gather(kv_local, "ctx", axis=1, tiled=True)
    full_out, full_in, full_down = gather(out_weight), gather(in_weight), gather(down_weight)
    attended, lse = fwd_call(lo, hi, query, kv_all, qmark, kmark, step)
    att_flat = attended.reshape(flat_count, width)
    inputs = inputs_half.astype(f32)
    residual = inputs + jnp.dot(att_flat, full_out, preferred_element_type=f32)
    normed_mlp, inverse_mlp = layer_norm(residual)
    act_mlp = (normed_mlp * mlp_gain.astype(f32)).astype(bf16)
    up_all = jnp.dot(act_mlp, full_in, preferred_element_type=f32)
    inner, gate = (up_all[:, :hidden], up_all[:, hidden:])
    gelu_value, gelu_slope = gelu_pair(inner)
    mixed = (gelu_value * gate).astype(bf16)
    output = (residual + jnp.dot(mixed, full_down, preferred_element_type=f32)).astype(bf16)
    cot_flat = cotangent.reshape(flat_count, width)
    d_mixed = matmul_back(cot_flat, full_down)
    d_up = jnp.concatenate([d_mixed * gate * gelu_slope, d_mixed * gelu_value], axis=-1).astype(
        bf16
    )
    local_down = token_grad(mixed, cot_flat)
    local_in = token_grad(act_mlp, d_up)
    d_act_mlp = matmul_back(d_up, full_in)
    local_mlp_gain = jnp.sum(d_act_mlp * normed_mlp, axis=0)
    d_residual = cot_flat.astype(f32) + norm_back(
        d_act_mlp * mlp_gain.astype(f32), normed_mlp, inverse_mlp
    )
    d_res_half = d_residual.astype(bf16)
    local_out = token_grad(att_flat, d_res_half)
    d_att = matmul_back(d_res_half, full_out).astype(bf16).reshape(shaped)
    early_in, early_out, early_down = scatter(local_in), scatter(local_out), scatter(local_down)
    grad_in = replica_sum(early_in)
    grad_out = replica_sum(early_out)
    grad_down = replica_sum(early_down)
    d_query, pair_terms = bwd_call(
        lo, hi, query, kv_all, qmark, kmark, d_att, attended, lse,
        cosine.reshape(rows_here, block_len, PAIR), sine.reshape(rows_here, block_len, PAIR), step,
    )
    if ctx_size == 2:
        mine = lax.dynamic_slice_in_dim(pair_terms, first_pos, block_len, 2)
        theirs = lax.dynamic_slice_in_dim(pair_terms, block_len - first_pos, block_len, 2)
        sides = [mine, lax.ppermute(theirs, "ctx", [(0, 1), (1, 0)])]
    else:
        sides = [lax.psum_scatter(pair_terms, "ctx", scatter_dimension=2, tiled=True)]
    sides = [s.reshape(2, flat_count, width) for s in sides]
    d_qkv = join_call(d_query.reshape(flat_count, width), cosine, sine, sides)
    local_qkv = token_grad(act_attn, d_qkv)
    grad_qkv = replica_sum(scatter(local_qkv))
    d_act_attn = matmul_back(d_qkv, full_qkv)
    normed_attn, inverse_attn = layer_norm(inputs)
    local_attn_gain = jnp.sum(d_act_attn * normed_attn, axis=0)
    input_grad = d_residual + norm_back(
        d_act_attn * attn_gain.astype(f32), normed_attn, inverse_attn
    )
    gains = lax.psum(jnp.stack([local_attn_gain, local_mlp_gain]), ("fsdp", "rep", "ctx"))
    grad_attn_gain, grad_mlp_gain = gains[0], gains[1]
    return (
        output.reshape(shaped),
        input_grad.reshape(shaped),
        grad_attn_gain,
        grad_qkv,
        grad_out,
        grad_mlp_gain,
        grad_in,
        grad_down,
    )


def solution(mesh):
    return jax.shard_map(
        functools.partial(per_device, dict(mesh.shape)),
        mesh=mesh,
        in_specs=(
            P(("fsdp", "rep"), "ctx", None),
            P(("fsdp", "rep"), "ctx", None),
            P(("fsdp", "rep"), None),
            P(),
            P("fsdp", None),
            P("fsdp", None),
            P(),
            P("fsdp", None),
            P("fsdp", None),
        ),
        out_specs=(
            P(("fsdp", "rep"), "ctx", None),
            P(("fsdp", "rep"), "ctx", None),
            P(),
            P("fsdp", None),
            P("fsdp", None),
            P(),
            P("fsdp", None),
            P("fsdp", None),
        ),
        check_vma=False,
    )
```

```python
import functools

import jax
import jax.numpy as jnp
from jax import lax
from jax.experimental import pallas as pl
from jax.experimental.pallas import tpu as pltpu
from jax.sharding import PartitionSpec as P

HD = 64
PAIR = 2 * HD

norm_eps = 1e-05
rope_base = 160000.0
masked_score = -1e30
QB = 512
KB = 512
bf16 = jnp.bfloat16
f32 = jnp.float32
NT = (((1,), (1,)), ((), ()))


def params(count):
    return pltpu.CompilerParams(
        dimension_semantics=("arbitrary",) * count, vmem_limit_bytes=56 * 1024 * 1024
    )


def layer_norm(values):
    center = values - jnp.mean(values, axis=-1, keepdims=True)
    inverse = lax.rsqrt(jnp.mean(center * center, axis=-1, keepdims=True) + norm_eps)
    return (center * inverse, inverse)


def norm_back(grad_normed, normed, inverse):
    mean_grad = jnp.mean(grad_normed, axis=-1, keepdims=True)
    mean_cross = jnp.mean(grad_normed * normed, axis=-1, keepdims=True)
    return (grad_normed - mean_grad - normed * mean_cross) * inverse


def gelu_pair(values):
    cumulative = 0.5 * (1.0 + lax.erf(values * 0.7071067811865476))
    density = jnp.exp(-0.5 * values * values) * 0.3989422804014327
    return (values * cumulative, cumulative + values * density)


def doc_tables(lengths, positions):
    doc_ends = jnp.cumsum(lengths)
    before = (doc_ends[None, :] <= positions[:, None]).astype(jnp.int32)
    segment = jnp.sum(before, axis=1)
    begins = jnp.sum(before * lengths[None, :], axis=1)
    return (segment, positions - begins)


def rope_lanes(offsets):
    lane = jnp.arange(PAIR, dtype=jnp.int32) % HD
    frequency = rope_base ** (-((lane % (HD // 2)).astype(f32) * (2.0 / HD)))
    angles = offsets.astype(f32)[:, None] * frequency
    sign = jnp.where(lane < HD // 2, -1.0, 1.0).astype(f32)
    return (jnp.cos(angles), jnp.sin(angles) * sign)


def swap_halves(values):
    lane = lax.broadcasted_iota(jnp.int32, values.shape, 1)
    front = (lane % HD) < HD // 2
    return jnp.where(
        front,
        pltpu.roll(values, PAIR - HD // 2, 1),
        pltpu.roll(values, HD // 2, 1),
    )


def qkv_kernel(x_ref, gain_ref, cos_ref, sin_ref, w_ref, act_ref, q_ref, kv_ref):
    width = x_ref.shape[1]
    normed, _ = layer_norm(x_ref[...].astype(f32))
    act = (normed * gain_ref[...].astype(f32)).astype(bf16)
    act_ref[...] = act
    cosine, sine = cos_ref[...], sin_ref[...]
    for start in range(0, 3 * width, 2 * PAIR):
        part = jnp.dot(act, w_ref[:, start : start + 2 * PAIR], preferred_element_type=f32)
        for half in range(2):
            at = start + half * PAIR
            piece = part[:, half * PAIR : (half + 1) * PAIR]
            if at < 2 * width:
                piece = piece * cosine + swap_halves(piece) * sine
            if at < width:
                q_ref[:, at : at + PAIR] = piece.astype(bf16)
            else:
                kv_ref[:, at - width : at - width + PAIR] = piece.astype(bf16)


def qkv_call(inputs, gain, cosine, sine, weight):
    count, width = inputs.shape
    rows = min(256, count)
    row = lambda n: pl.BlockSpec((rows, n), lambda i: (i, 0))
    whole = lambda a: pl.BlockSpec(a.shape, lambda i: (0, 0))
    return pl.pallas_call(
        qkv_kernel,
        grid=(count // rows,),
        in_specs=[row(width), whole(gain), row(PAIR), row(PAIR), whole(weight)],
        out_specs=[row(width), row(width), row(2 * width)],
        out_shape=[
            jax.ShapeDtypeStruct((count, width), bf16),
            jax.ShapeDtypeStruct((count, width), bf16),
            jax.ShapeDtypeStruct((count, 2 * width), bf16),
        ],
        compiler_params=params(1),
        cost_estimate=pl.CostEstimate(
            flops=6 * count * width * width, bytes_accessed=12 * 1024 * 1024, transcendentals=0
        ),
    )(inputs, gain, cosine, sine, weight)


def split_heads(values, mark):
    lane = lax.broadcasted_iota(jnp.int32, values.shape, 1)
    zero = jnp.zeros_like(values)
    front, back = jnp.where(lane < HD, values, zero), jnp.where(lane < HD, zero, values)
    if mark is None:
        return front, back
    return jnp.concatenate([front, mark], axis=1), jnp.concatenate([back, mark], axis=1)


def fwd_kernel(step, lo_ref, hi_ref, q_ref, k_ref, v_ref, qm_ref, km_ref, o_ref, lse_ref, vt_ref):
    r, block = pl.program_id(0), pl.program_id(2)
    scale = HD ** (-0.5)

    @pl.when(block == 0)
    def _():
        for i in range(vt_ref.shape[0]):
            vt_ref[i] = v_ref[0, i * step : (i + 1) * step, :].T

    queries = split_heads((q_ref[0].astype(f32) * scale).astype(bf16), qm_ref[0])
    count = q_ref.shape[1]

    def body(index, carry):
        rows = pl.ds(pl.multiple_of(index * step, step), step)
        keys = jnp.concatenate([k_ref[0, rows, :], km_ref[0, rows, :]], axis=1)
        turned = vt_ref[index]
        result = []
        for h in range(2):
            run_max, run_sum, accum = carry[h]
            scores = lax.dot_general(keys, queries[h], NT, preferred_element_type=f32)
            new_max = jnp.maximum(run_max, jnp.max(scores, axis=0, keepdims=True))
            weights = jnp.exp(scores - new_max)
            factor = jnp.exp(run_max - new_max)
            new_sum = run_sum * factor + jnp.sum(weights, axis=0, keepdims=True)
            new_acc = accum * factor + jnp.dot(
                turned[h * HD : (h + 1) * HD], weights.astype(bf16), preferred_element_type=f32
            )
            result.append((new_max, new_sum, new_acc))
        return tuple(result)

    one = (
        jnp.full((1, count), masked_score, f32),
        jnp.zeros((1, count), f32),
        jnp.zeros((HD, count), f32),
    )
    state = lax.fori_loop(lo_ref[r, block], hi_ref[r, block], body, (one, one))
    outs = []
    for h in range(2):
        run_max, run_sum, accum = state[h]
        lse_ref[0, 0, h : h + 1, :] = run_max + jnp.log(run_sum)
        outs.append(accum / run_sum)
    o_ref[0] = jnp.concatenate(outs, axis=0).T.astype(bf16)


def fwd_call(lo, hi, query, kv, qmark, kmark, step):
    rows_here, count, width = query.shape
    length = kv.shape[1]
    pairs = width // PAIR
    qb = count // lo.shape[1]
    qspec = pl.BlockSpec((1, qb, PAIR), lambda r, h, i, *_: (r, i, h))
    return pl.pallas_call(
        functools.partial(fwd_kernel, step),
        grid_spec=pltpu.PrefetchScalarGridSpec(
            num_scalar_prefetch=2,
            grid=(rows_here, pairs, count // qb),
            in_specs=[
                qspec,
                pl.BlockSpec((1, length, PAIR), lambda r, h, i, *_: (r, 0, h)),
                pl.BlockSpec((1, length, PAIR), lambda r, h, i, *_: (r, 0, h + pairs)),
                pl.BlockSpec((1, qb, PAIR), lambda r, h, i, *_: (r, i, 0)),
                pl.BlockSpec((1, length, PAIR), lambda r, h, i, *_: (r, 0, 0)),
            ],
            out_specs=[
                qspec,
                pl.BlockSpec((1, 1, 2, qb), lambda r, h, i, *_: (r, h, 0, i)),
            ],
            scratch_shapes=[pltpu.VMEM((length // step, PAIR, step), bf16)],
        ),
        out_shape=[
            jax.ShapeDtypeStruct(query.shape, bf16),
            jax.ShapeDtypeStruct((rows_here, pairs, 2, count), f32),
        ],
        compiler_params=params(3),
        cost_estimate=pl.CostEstimate(
            flops=rows_here * 48 * count * length * width,
            bytes_accessed=16 * 1024 * 1024,
            transcendentals=0,
        ),
    )(lo, hi, query, kv, kv, qmark, kmark)


def bwd_kernel(
    step, lo_ref, hi_ref, first_ref, q_ref, k_ref, v_ref, qm_ref, km_ref, do_ref, o_ref, lse_ref,
    cos_ref, sin_ref, dq_ref, *rest,
):
    sides, (kt_ref, dk_acc, dv_acc) = rest[:-3], rest[-3:]
    r, block = pl.program_id(0), pl.program_id(2)
    scale = HD ** (-0.5)

    @pl.when(block == 0)
    def _():
        for i in range(kt_ref.shape[0]):
            kt_ref[i] = k_ref[0, i * step : (i + 1) * step, :].T
        dk_acc[...] = jnp.zeros_like(dk_acc)
        dv_acc[...] = jnp.zeros_like(dv_acc)

    count = q_ref.shape[1]
    scaled = (q_ref[0].astype(f32) * scale).astype(bf16)
    queries = split_heads(scaled, qm_ref[0])
    query_rows = jnp.concatenate(split_heads(scaled, None), axis=0)
    grads = split_heads(do_ref[0], None)
    grad_rows = jnp.concatenate(grads, axis=0)
    products = (do_ref[0].astype(f32) * o_ref[0].astype(f32)).T
    deltas = [jnp.sum(products[h * HD : (h + 1) * HD], axis=0, keepdims=True) for h in range(2)]
    totals = [lse_ref[0, 0, h : h + 1, :] for h in range(2)]

    def body(index, carry):
        rows = pl.ds(pl.multiple_of(index * step, step), step)
        keys = jnp.concatenate([k_ref[0, rows, :], km_ref[0, rows, :]], axis=1)
        values = v_ref[0, rows, :]
        turned = kt_ref[index]
        result, probs_all, ds_all = [], [], []
        for h in range(2):
            scores = lax.dot_general(keys, queries[h], NT, preferred_element_type=f32)
            probs = jnp.exp(scores - totals[h])
            d_probs = lax.dot_general(values, grads[h], NT, preferred_element_type=f32)
            d_scores = (probs * (d_probs - deltas[h])).astype(bf16)
            result.append(
                carry[h]
                + jnp.dot(turned[h * HD : (h + 1) * HD], d_scores, preferred_element_type=f32)
            )
            probs_all.append(probs.astype(bf16))
            ds_all.append(d_scores)
        dv_acc[rows, :] += jnp.dot(
            jnp.concatenate(probs_all, axis=1), grad_rows, preferred_element_type=f32
        )
        dk_acc[rows, :] += jnp.dot(
            jnp.concatenate(ds_all, axis=1), query_rows, preferred_element_type=f32
        )
        return tuple(result)

    zero = jnp.zeros((HD, count), f32)
    state = lax.fori_loop(lo_ref[r, block], hi_ref[r, block], body, (zero, zero))
    d_query = jnp.concatenate(state, axis=0).T * scale
    d_query = d_query * cos_ref[0] - swap_halves(d_query) * sin_ref[0]
    dq_ref[0] = d_query.astype(bf16)

    @pl.when(block == pl.num_programs(2) - 1)
    def _():
        for index, side in enumerate(sides):
            size = side.shape[2]
            start = pl.multiple_of(lax.rem(first_ref[0] + index * size, dk_acc.shape[0]), size)
            side[0, 0] = dk_acc[pl.ds(start, size), :].astype(bf16)
            side[1, 0] = dv_acc[pl.ds(start, size), :].astype(bf16)


def bwd_call(lo, hi, first, parts, query, kv, qmark, kmark, d_att, att, lse, cosine, sine, step):
    rows_here, count, width = query.shape
    length = kv.shape[1]
    pairs = width // PAIR
    qb = count // lo.shape[1]
    qspec = pl.BlockSpec((1, qb, PAIR), lambda r, h, i, *_: (r, i, h))
    tspec = pl.BlockSpec((1, qb, PAIR), lambda r, h, i, *_: (r, i, 0))
    return pl.pallas_call(
        functools.partial(bwd_kernel, step),
        grid_spec=pltpu.PrefetchScalarGridSpec(
            num_scalar_prefetch=3,
            grid=(rows_here, pairs, count // qb),
            in_specs=[
                qspec,
                pl.BlockSpec((1, length, PAIR), lambda r, h, i, *_: (r, 0, h)),
                pl.BlockSpec((1, length, PAIR), lambda r, h, i, *_: (r, 0, h + pairs)),
                tspec,
                pl.BlockSpec((1, length, PAIR), lambda r, h, i, *_: (r, 0, 0)),
                qspec,
                qspec,
                pl.BlockSpec((1, 1, 2, qb), lambda r, h, i, *_: (r, h, 0, i)),
                tspec,
                tspec,
            ],
            out_specs=[
                qspec,
            ]
            + [pl.BlockSpec((2, 1, length // parts, PAIR), lambda r, h, i, *_: (0, r, 0, h))]
            * parts,
            scratch_shapes=[
                pltpu.VMEM((length // step, PAIR, step), bf16),
                pltpu.VMEM((length, PAIR), f32),
                pltpu.VMEM((length, PAIR), f32),
            ],
        ),
        out_shape=[
            jax.ShapeDtypeStruct(query.shape, bf16),
        ]
        + [jax.ShapeDtypeStruct((2, rows_here, length // parts, width), bf16)] * parts,
        compiler_params=params(3),
        cost_estimate=pl.CostEstimate(
            flops=rows_here * 50 * count * length * width,
            bytes_accessed=24 * 1024 * 1024,
            transcendentals=0,
        ),
    )(lo, hi, first, query, kv, kv, qmark, kmark, d_att, att, lse, cosine, sine)


def join_kernel(parts, *refs):
    dq_ref, cos_ref, sin_ref = refs[:3]
    sides, out_ref = refs[3:-1], refs[-1]
    width = dq_ref.shape[1]
    out_ref[:, :width] = dq_ref[...]
    for at in range(0, width, PAIR):
        lanes = slice(at, at + PAIR)
        d_key = sum(s[0, :, lanes].astype(f32) for s in sides)
        d_key = d_key * cos_ref[...] - swap_halves(d_key) * sin_ref[...]
        out_ref[:, width + at : width + at + PAIR] = d_key.astype(bf16)
        d_value = sum(s[1, :, lanes].astype(f32) for s in sides)
        out_ref[:, 2 * width + at : 2 * width + at + PAIR] = d_value.astype(bf16)


def join_call(dq, cosine, sine, sides):
    count, width = dq.shape
    rows = min(256, count)
    row = lambda n: pl.BlockSpec((rows, n), lambda i: (i, 0))
    return pl.pallas_call(
        functools.partial(join_kernel, len(sides)),
        grid=(count // rows,),
        in_specs=[row(width), row(PAIR), row(PAIR)]
        + [pl.BlockSpec((2, rows, width), lambda i: (0, i, 0))] * len(sides),
        out_specs=row(3 * width),
        out_shape=jax.ShapeDtypeStruct((count, 3 * width), bf16),
        compiler_params=params(1),
        cost_estimate=pl.CostEstimate(
            flops=count * width * 10, bytes_accessed=12 * 1024 * 1024, transcendentals=0
        ),
    )(dq, cosine, sine, *sides)


def token_grad(activations, gradient):
    return lax.dot_general(
        activations, gradient, (((0,), (0,)), ((), ())), preferred_element_type=f32
    ).astype(bf16)


def matmul_back(gradient, weight):
    return lax.dot_general(gradient, weight, NT, preferred_element_type=f32)


def per_device(
    sizes,
    tokens,
    cotangent,
    doc_lengths,
    attn_gain,
    qkv_weight,
    out_weight,
    mlp_gain,
    in_weight,
    down_weight,
):
    rows_here, block_len, width = tokens.shape
    ctx_size = sizes["ctx"]
    length = block_len * ctx_size
    flat_count = rows_here * block_len
    hidden = down_weight.shape[0] * sizes["fsdp"]
    docs = doc_lengths.shape[1]
    paired = (
        ctx_size == 2
        and sizes["rep"] == 2
        and sizes["fsdp"] >= 2
        and sizes["fsdp"] & (sizes["fsdp"] - 1) == 0
    )
    ctx_index = lax.axis_index("ctx")

    def pair_sum(value, axis):
        if sizes[axis] == 2:
            other = lax.ppermute(value, axis, [(0, 1), (1, 0)])
            return value.astype(f32) + other.astype(f32)
        return lax.psum(value, axis).astype(f32)

    def gather(*weights):
        if not paired:
            return [lax.all_gather(w, "fsdp", axis=0, tiled=True) for w in weights]
        halves = [w.shape[1] // 2 for w in weights]
        mine = [
            lax.dynamic_slice_in_dim(w, ctx_index * half, half, 1)
            for w, half in zip(weights, halves)
        ]
        mine = jnp.concatenate(mine, axis=1) if len(mine) > 1 else mine[0]
        mine = lax.all_gather(mine, "fsdp", axis=0, tiled=True)
        left, right = in_order(mine, swap(mine, "ctx", 1), "ctx")
        at, result = 0, []
        for half in halves:
            result.append(
                jnp.concatenate([left[:, at : at + half], right[:, at : at + half]], axis=1)
            )
            at += half
        return result

    def swap(value, axis, bit):
        return lax.ppermute(value, axis, [(i, i ^ bit) for i in range(sizes[axis])])

    def in_order(mine, other, axis):
        first = lax.axis_index(axis) == 0
        return jnp.where(first, mine, other), jnp.where(first, other, mine)

    def halve(value, axis, bit, dim):
        size = value.shape[dim] // 2
        me = (lax.axis_index(axis) // bit) % 2
        mine = lax.dynamic_slice_in_dim(value, me * size, size, dim)
        theirs = lax.dynamic_slice_in_dim(value, (1 - me) * size, size, dim)
        return (mine.astype(f32) + swap(theirs, axis, bit).astype(f32)).astype(bf16)

    def to_owner(value, low_bits):
        rest = sizes["fsdp"] // low_bits
        bit = rest // 2
        while bit >= 1:
            value = halve(value, "fsdp", bit * low_bits, 0)
            bit //= 2
        return value[0]

    def split_low(value):
        owners, rows, cols = value.shape
        value = value.reshape(owners // 2, 2, rows, cols)
        return halve(value, "fsdp", 1, 1).reshape(owners // 2, rows, cols)

    def split_rep(value):
        return halve(value, "rep", 1, 1)

    def tree_sum(grad):
        rows, cols = grad.shape
        grad = halve(grad, "ctx", 1, 1)
        owners = sizes["fsdp"]
        grad = grad.reshape(owners, rows // owners, cols // 2)
        cut = -(-cols // 4 // 128) * 128
        one, two = grad[:, :, :cut], grad[:, :, cut:]
        one, two = split_rep(one), split_low(two)
        one, two = split_low(one), split_rep(two)
        one, two = to_owner(one, 2), to_owner(two, 2)
        mine = jnp.concatenate([one, two], axis=1)
        mine = jnp.concatenate(in_order(mine, swap(mine, "rep", 1), "rep"), axis=0)
        return jnp.concatenate(in_order(mine, swap(mine, "ctx", 1), "ctx"), axis=1).astype(f32)

    def queue_sum(grads):
        if not paired:
            return [replica_sum(scatter(g)) for g in grads]
        halves = [g.shape[1] // 2 for g in grads]
        merged = [halve(g, "ctx", 1, 1) for g in grads]
        merged = jnp.concatenate(merged, axis=1) if len(merged) > 1 else merged[0]
        shard = scatter(merged)
        shard = (shard.astype(f32) + swap(shard, "rep", 1).astype(f32)).astype(bf16)
        left, right = in_order(shard, swap(shard, "ctx", 1), "ctx")
        at, result = 0, []
        for half in halves:
            both = [left[:, at : at + half], right[:, at : at + half]]
            result.append(jnp.concatenate(both, axis=1).astype(f32))
            at += half
        return result

    def total(value):
        if not paired:
            return lax.psum(value, ("fsdp", "rep", "ctx"))
        for axis in ("ctx", "rep", "fsdp"):
            bit = 1
            while bit < sizes[axis]:
                value = value + swap(value, axis, bit)
                bit *= 2
        return value

    def scatter(grad):
        return lax.psum_scatter(grad, "fsdp", scatter_dimension=0, tiled=True)

    def replica_sum(shard):
        return pair_sum(pair_sum(shard, "ctx").astype(bf16), "rep")

    first_pos = ctx_index * block_len
    local_pos = first_pos + jnp.arange(block_len, dtype=jnp.int32)
    all_pos = jnp.arange(length, dtype=jnp.int32)
    seg_all, _ = jax.vmap(doc_tables, in_axes=(0, None))(doc_lengths, all_pos)
    seg_query, offsets = jax.vmap(doc_tables, in_axes=(0, None))(doc_lengths, local_pos)
    cosine, sine = rope_lanes(offsets.reshape(flat_count))
    lane = jnp.arange(PAIR, dtype=jnp.int32)
    qmark = (seg_query[:, :, None] == lane).astype(bf16)
    kmark = jnp.where(
        (seg_all[:, :, None] != lane) & (lane < docs), masked_score, 0.0
    ).astype(bf16)
    qb = min(QB, block_len)
    step = min(KB, length)
    ends = jnp.cumsum(doc_lengths, axis=1)
    low_pos = first_pos + jnp.arange(block_len // qb, dtype=jnp.int32) * qb
    high_pos = low_pos + qb - 1
    past = lambda pos: ends[:, None, :] <= pos[None, :, None]
    lo = jnp.max(jnp.where(past(low_pos), ends[:, None, :], 0), axis=-1) // step
    hi = jnp.min(jnp.where(past(high_pos), length, ends[:, None, :]), axis=-1)
    hi = (hi + step - 1) // step

    inputs_half = tokens.reshape(flat_count, width)
    (full_qkv,) = gather(qkv_weight)
    act_attn, query, kv_local = qkv_call(
        inputs_half, attn_gain.reshape(1, width), cosine, sine, full_qkv
    )
    shaped = (rows_here, block_len, width)
    query = query.reshape(shaped)
    kv_local = kv_local.reshape(rows_here, block_len, 2 * width)
    if ctx_size == 2:
        kv_other = lax.ppermute(kv_local, "ctx", [(0, 1), (1, 0)])
        first = ctx_index == 0
        kv_all = jnp.concatenate(
            [jnp.where(first, kv_local, kv_other), jnp.where(first, kv_other, kv_local)], axis=1
        )
    else:
        kv_all = lax.all_gather(kv_local, "ctx", axis=1, tiled=True)
    full_out, full_in = gather(out_weight, in_weight)
    (full_down,) = gather(down_weight)
    attended, lse = fwd_call(lo, hi, query, kv_all, qmark, kmark, step)
    att_flat = attended.reshape(flat_count, width)
    inputs = inputs_half.astype(f32)
    residual = inputs + jnp.dot(att_flat, full_out, preferred_element_type=f32)
    normed_mlp, inverse_mlp = layer_norm(residual)
    act_mlp = (normed_mlp * mlp_gain.astype(f32)).astype(bf16)
    up_all = jnp.dot(act_mlp, full_in, preferred_element_type=f32)
    inner, gate = (up_all[:, :hidden], up_all[:, hidden:])
    gelu_value, gelu_slope = gelu_pair(inner)
    mixed = (gelu_value * gate).astype(bf16)
    output = (residual + jnp.dot(mixed, full_down, preferred_element_type=f32)).astype(bf16)
    cot_flat = cotangent.reshape(flat_count, width)
    d_mixed = matmul_back(cot_flat, full_down)
    d_up = jnp.concatenate([d_mixed * gate * gelu_slope, d_mixed * gelu_value], axis=-1).astype(
        bf16
    )
    local_down = token_grad(mixed, cot_flat)
    local_in = token_grad(act_mlp, d_up)
    d_act_mlp = matmul_back(d_up, full_in)
    local_mlp_gain = jnp.sum(d_act_mlp * normed_mlp, axis=0)
    d_residual = cot_flat.astype(f32) + norm_back(
        d_act_mlp * mlp_gain.astype(f32), normed_mlp, inverse_mlp
    )
    d_res_half = d_residual.astype(bf16)
    local_out = token_grad(att_flat, d_res_half)
    d_att = matmul_back(d_res_half, full_out).astype(bf16).reshape(shaped)
    (grad_down,) = queue_sum([local_down])
    grad_in, grad_out = queue_sum([local_in, local_out])
    start = first_pos.reshape(1) if ctx_size == 2 else jnp.zeros((1,), jnp.int32)
    d_query, *sides = bwd_call(
        lo, hi, start.astype(jnp.int32), 2 if ctx_size == 2 else 1, query, kv_all, qmark, kmark, d_att, attended, lse,
        cosine.reshape(rows_here, block_len, PAIR), sine.reshape(rows_here, block_len, PAIR), step,
    )
    if ctx_size == 2:
        sides = [sides[0], swap(sides[1], "ctx", 1)]
    else:
        sides = [lax.psum_scatter(sides[0], "ctx", scatter_dimension=2, tiled=True)]
    sides = [s.reshape(2, flat_count, width) for s in sides]
    d_qkv = join_call(d_query.reshape(flat_count, width), cosine, sine, sides)
    local_qkv = token_grad(act_attn, d_qkv)
    grad_qkv = tree_sum(local_qkv) if paired else replica_sum(scatter(local_qkv))
    d_act_attn = matmul_back(d_qkv, full_qkv)
    normed_attn, inverse_attn = layer_norm(inputs)
    local_attn_gain = jnp.sum(d_act_attn * normed_attn, axis=0)
    input_grad = d_residual + norm_back(
        d_act_attn * attn_gain.astype(f32), normed_attn, inverse_attn
    )
    gains = total(jnp.stack([local_attn_gain, local_mlp_gain]))
    grad_attn_gain, grad_mlp_gain = gains[0], gains[1]
    return (
        output.reshape(shaped),
        input_grad.reshape(shaped),
        grad_attn_gain,
        grad_qkv,
        grad_out,
        grad_mlp_gain,
        grad_in,
        grad_down,
    )


def solution(mesh):
    return jax.shard_map(
        functools.partial(per_device, dict(mesh.shape)),
        mesh=mesh,
        in_specs=(
            P(("fsdp", "rep"), "ctx", None),
            P(("fsdp", "rep"), "ctx", None),
            P(("fsdp", "rep"), None),
            P(),
            P("fsdp", None),
            P("fsdp", None),
            P(),
            P("fsdp", None),
            P("fsdp", None),
        ),
        out_specs=(
            P(("fsdp", "rep"), "ctx", None),
            P(("fsdp", "rep"), "ctx", None),
            P(),
            P("fsdp", None),
            P("fsdp", None),
            P(),
            P("fsdp", None),
            P("fsdp", None),
        ),
        check_vma=False,
    )
```
